256 devices in a mesh: sub: 64 (over x, z_lo, y, core), chan: 4 (over z_hi).
Axes of the slice: x: 4, y: 4, z: 8 (z_hi: 4, z_lo: 2; z = z_hi * 2 + z_lo), core: 2. Of those that a mesh axis runs over, the one named last changes fastest.
Arguments:
- echoes: bfloat16 [2, 8, 16384, 1024], P(None, 'chan', 'sub'), may hold values from -6 to 6
- angle_offsets: int32 [64, 3, 2, 256], P('sub'), may hold values from 0 to 224
- angle_coefs: float32 [64, 3, 2, 32, 256], P('sub'), may hold values from -0.875 to 0.875
- range_offsets: int32 [64, 3, 2, 1024], P('sub'), may hold values from 0 to 992
- range_coefs: float32 [64, 3, 2, 32, 1024], P('sub'), may hold values from -0.875 to 0.875
- beam_phase: float32 [64, 3, 2, 256], P('sub'), may hold values from -3.140625 to 3.140625
- range_phase: float32 [8, 3, 2, 1024], P('chan'), may hold values from -3.140625 to 3.140625
Outputs:
- image: float32 [2, 16384, 1024], P(None, 'sub', 'chan')
The draws below stay inside these ranges and needn't reach their ends.
All inputs are finite; a program needn't handle non-finite values.
Results may differ from the reference program's by a relative error of at most 0.0094.
Values may be sent and summed in bfloat16 or wider, within the bound.
No kernel may reach another device: no remote copies, remote signals or barrier semaphores. Data moves between devices by JAX's collectives and lax.ppermute only.
A program may use at most 64 MiB of HBM per device.

```python
import jax
import jax.numpy as jnp
from jax import lax

B = 256
R = 1024
TAPS = 32
SECTIONS = 3
NSUB = 64
CHANNELS = 8
N_SUB = 64


def touch_ends(drawn, own_key, smallest, top_value):
    spot = [jax.random.randint(jax.random.fold_in(own_key, axis), (), 0, length) for axis, length in enumerate(drawn.shape)]
    longest = drawn.shape.index(max(drawn.shape))
    neighbour = spot[:longest] + [(spot[longest] + 1) % drawn.shape[longest]] + spot[longest + 1:]
    return drawn.at[tuple(spot)].set(smallest).at[tuple(neighbour)].set(top_value)


def block_scale(own_key, shape, shards, smallest, top_value):
    factor_of, own = 1.0, jax.random.fold_in(own_key, 6)
    for dim, shards_of in shards:
        draws = jnp.exp(jax.random.uniform(jax.random.fold_in(own, dim), (shards_of,), jnp.float32, smallest / len(shards), top_value / len(shards)))
        factor_of = factor_of * jnp.repeat(draws, shape[dim] // shards_of).reshape([-1 if axis == dim else 1 for axis in range(len(shape))])
    return factor_of


def noise(stream_key, shape, deviation, limit, pieces=(), held_as=jnp.bfloat16):
    loudness = block_scale(stream_key, shape, pieces, -0.22, 0.18) if pieces else 1.0
    result = jax.random.normal(stream_key, shape, jnp.float32) * deviation * loudness
    return jnp.minimum(jnp.maximum(result, -limit), limit).astype(held_as)


def setup_inputs(seed: int = 0) -> dict:
    streams_of = jax.random.split(jax.random.key(seed), 8)
    return {
        "echoes": noise(streams_of[0], (2, CHANNELS, NSUB * B, R), 1.0, 6.0, ((1, 4), (2, 64))),
        "angle_offsets": touch_ends(jax.random.randint(streams_of[1], (NSUB, SECTIONS, 2, B), 0, B - TAPS + 1), jax.random.fold_in(streams_of[1], 1), 0, B - TAPS).astype(jnp.int32),
        "angle_coefs": noise(streams_of[2], (NSUB, SECTIONS, 2, TAPS, B), 45 ** -0.5, 0.875, ((0, 64),), jnp.float32),
        "range_offsets": touch_ends(jax.random.randint(streams_of[3], (NSUB, SECTIONS, 2, R), 0, R - TAPS + 1), jax.random.fold_in(streams_of[3], 1), 0, R - TAPS).astype(jnp.int32),
        "range_coefs": noise(streams_of[4], (NSUB, SECTIONS, 2, TAPS, R), 45 ** -0.5, 0.875, ((0, 64),), jnp.float32),
        "beam_phase": jnp.clip(jax.random.uniform(streams_of[5], (NSUB, SECTIONS, 2, B), jnp.float32, -3.140625, 3.140625), -3.140625, 3.140625),
        "range_phase": jnp.clip(jax.random.uniform(streams_of[6], (CHANNELS, SECTIONS, 2, R), jnp.float32, -3.140625, 3.140625), -3.140625, 3.140625),
    }


def angle_matrix(offsets, coefs):
    taps = coefs.shape[0]
    beams = coefs.shape[1]
    distance = jnp.arange(beams, dtype=jnp.int32)[None, :] - offsets.astype(jnp.int32)[:, None]
    inside = (distance >= 0) & (distance < taps)
    picked = jnp.take_along_axis(coefs.T, jnp.clip(distance, 0, taps - 1), axis=1)
    return jnp.where(inside, picked, jnp.zeros_like(picked)).astype(jnp.bfloat16)


def range_matrix(offsets, coefs):
    taps = coefs.shape[0]
    bins = coefs.shape[1]
    distance = jnp.arange(bins, dtype=jnp.int32)[:, None] - offsets.astype(jnp.int32)[None, :]
    inside = (distance >= 0) & (distance < taps)
    picked = jnp.take_along_axis(coefs, jnp.clip(distance, 0, taps - 1), axis=0)
    return jnp.where(inside, picked, jnp.zeros_like(picked)).astype(jnp.bfloat16)


def contribute(block, offsets_a, coefs_a, offsets_r, coefs_r, beam_angle, channel_angle):
    angle_mat = angle_matrix(offsets_a, coefs_a)
    range_mat = range_matrix(offsets_r, coefs_r)
    mixed = jnp.einsum("ab,pcbr->pcar", angle_mat.astype(jnp.float32), block.astype(jnp.float32)).astype(jnp.bfloat16)
    bins = range_mat.shape[0]
    filtered = jnp.dot(mixed.reshape(-1, bins), range_mat, preferred_element_type=jnp.float32).reshape(mixed.shape)
    rotation = beam_angle[None, :, None] + channel_angle[:, None, :]
    cosine = jnp.cos(rotation)
    sine = jnp.sin(rotation)
    real_part = filtered[0] * cosine - filtered[1] * sine
    imag_part = filtered[0] * sine + filtered[1] * cosine
    return jnp.stack([real_part, imag_part])


def reference(echoes, angle_offsets, angle_coefs, range_offsets, range_coefs, beam_phase, range_phase):
    blocks = N_SUB
    levels = blocks.bit_length() - 1
    bins = echoes.shape[3]
    current = echoes.reshape(2, CHANNELS, blocks, B, bins)
    image = None
    for section_num in range(SECTIONS):
        bit_pos = levels - 1 - section_num
        final = section_num == SECTIONS - 1

        def one_block(device):
            own_bit = (device >> bit_pos) & 1
            base_block = (device - own_bit * (1 << bit_pos)).astype(jnp.int32)
            merged = jnp.zeros((2, CHANNELS, B, bins), jnp.float32)
            for side_num in range(2):
                source = (base_block + side_num * (1 << bit_pos)).astype(jnp.int32)
                block = lax.dynamic_index_in_dim(current, source, 2, keepdims=False)
                merged = merged + contribute(
                    block,
                    angle_offsets[device, section_num, side_num],
                    angle_coefs[device, section_num, side_num],
                    range_offsets[device, section_num, side_num],
                    range_coefs[device, section_num, side_num],
                    beam_phase[device, section_num, side_num],
                    range_phase[:, section_num, side_num],
                )
            if final:
                return jnp.sum(merged, axis=1)
            return merged.astype(jnp.bfloat16)

        results = lax.map(one_block, jnp.arange(blocks, dtype=jnp.int32))
        if final:
            image = jnp.transpose(results, (1, 0, 2, 3)).reshape(2, blocks * B, bins)
        else:
            current = jnp.transpose(results, (1, 2, 0, 3, 4))
    return image
```

```python
import functools

import jax
import jax.numpy as jnp
from jax import lax
from jax.experimental import pallas as pl
from jax.experimental.pallas import tpu as pltpu
from jax.sharding import PartitionSpec as P


F32 = jnp.float32
BF16 = jnp.bfloat16
TILE = 256
PACK_ROWS = 48


def partner_2(shard, axis, distance):
    return lax.ppermute(shard, axis, [(i, i ^ 1 << distance) for i in range(lax.axis_size(axis))])


def pack_kernel(rc_ref, ro_ref, ac_ref, ao_ref, bp_ref, out_ref):
    taps, bins = rc_ref.shape[1:]
    beams = ac_ref.shape[2]
    out_ref[0, :taps, :] = rc_ref[0].astype(BF16)
    ro = ro_ref[0]
    ao = ao_ref[0]
    beta = bp_ref[0]
    b1 = beta.astype(BF16).astype(F32)
    b2 = (beta - b1).astype(BF16).astype(F32)
    b3 = beta - b1 - b2
    r_hi, r_lo = (ro >> 5).astype(F32), (ro & 31).astype(F32)
    a_hi, a_lo = (ao >> 5).astype(F32), (ao & 31).astype(F32)
    row2 = jnp.concatenate([a_hi, a_lo, b1, b2], axis=1)
    row3 = jnp.concatenate([b3, jnp.zeros((1, bins - beams), F32)], axis=1)
    spot = lax.broadcasted_iota(jnp.int32, (8, bins), 0)
    head = jnp.where(spot == 0, r_hi, jnp.where(spot == 1, r_lo, jnp.where(spot == 2, row2, row3)))
    angle = jnp.concatenate([ac_ref[0, 8 * g:8 * g + 8, :] for g in range(4)], axis=1)
    out_ref[0, taps:, :] = jnp.concatenate([head, angle], axis=0).astype(BF16)


def pack_tables(range_coefs, range_offsets, angle_coefs, angle_offsets, beam_phase):
    sections, sides, taps, bins = range_coefs.shape[1:]
    beams = angle_coefs.shape[4]
    n = sections * sides
    args = (
        range_coefs.reshape(n, taps, bins),
        range_offsets.reshape(n, 1, bins),
        angle_coefs.reshape(n, taps, beams),
        angle_offsets.reshape(n, 1, beams),
        beam_phase.reshape(n, 1, beams),
    )
    packs = []
    for section in range(sections):
        packs.append(
            pl.pallas_call(
                pack_kernel,
                grid=(sides,),
                in_specs=[
                    pl.BlockSpec((1,) + a.shape[1:], lambda i, s=section: (s * sides + i, 0, 0))
                    for a in args
                ],
                out_specs=pl.BlockSpec((1, PACK_ROWS, bins), lambda i: (i, 0, 0)),
                out_shape=jax.ShapeDtypeStruct((sides, PACK_ROWS, bins), BF16),
                name="pack",
            )(*args)
        )
    return packs


def place(taps, hi, lo, blocks, store):
    window = jnp.concatenate([taps, jnp.zeros_like(taps)], axis=0)
    for bit in range(5):
        moved = pltpu.roll(window, 1 << bit, axis=0)
        window = jnp.where((lo >> bit) & 1 == 1, moved, window)
    first, second = window[:32], window[32:]
    hi = jnp.broadcast_to(hi, first.shape)
    zero = jnp.zeros_like(first)
    for k in range(blocks):
        rows = jnp.where(hi == k, first, jnp.where(hi == k - 1, second, zero))
        store(k, rows.astype(BF16))


def build_kernel(pack_ref, m_ref, at_ref, rot_ref):
    bins = m_ref.shape[2]
    beams = at_ref.shape[2]

    def columns(j, carry):
        lanes = pl.ds(pl.multiple_of(j * 128, 128), 128)
        taps = pack_ref[0, :32, lanes].astype(F32)
        head = pack_ref[0, 32:48, lanes].astype(F32)
        hi = head[0:1].astype(jnp.int32)
        lo = head[1:2].astype(jnp.int32)

        def store(k, rows):
            m_ref[0, 32 * k:32 * k + 32, lanes] = rows

        place(taps, hi, lo, bins // 32, store)
        return carry

    lax.fori_loop(0, bins // 128, columns, 0)

    tail = pack_ref[0, 32:48, :].astype(F32)
    angle = jnp.concatenate([tail[8:16, 256 * g:256 * g + 256] for g in range(4)], axis=0)
    a_hi = tail[2:3, 0:256].astype(jnp.int32)
    a_lo = tail[2:3, 256:512].astype(jnp.int32)

    def store_angle(k, rows):
        at_ref[0, 32 * k:32 * k + 32, :] = rows

    place(angle, a_hi, a_lo, beams // 32, store_angle)
    beta = tail[2:3, 512:768] + tail[2:3, 768:1024] + tail[3:4, 0:256]
    beta = jnp.broadcast_to(beta, (8, beams))
    for t, fn in enumerate((jnp.cos, jnp.sin)):
        wide = jnp.broadcast_to(fn(beta)[0:1], (128, beams))
        rot_ref[0, t] = wide.T


def build(pack):
    sides, rows, bins = pack.shape
    beams = 256
    return pl.pallas_call(
        build_kernel,
        grid=(sides,),
        in_specs=[pl.BlockSpec((1, rows, bins), lambda i: (i, 0, 0))],
        out_specs=[
            pl.BlockSpec((1, bins, bins), lambda i: (i, 0, 0)),
            pl.BlockSpec((1, beams, beams), lambda i: (i, 0, 0)),
            pl.BlockSpec((1, 2, beams, 128), lambda i: (i, 0, 0, 0)),
        ],
        out_shape=[
            jax.ShapeDtypeStruct((sides, bins, bins), BF16),
            jax.ShapeDtypeStruct((sides, beams, beams), BF16),
            jax.ShapeDtypeStruct((sides, 2, beams, 128), F32),
        ],
        name="build",
    )(pack)


def mix(sp_ref, x_refs, at_ref, mixed_ref):
    beams = at_ref.shape[1]
    for i, x_ref in enumerate(x_refs):
        side = i ^ sp_ref[0]
        at = at_ref[side]
        for part in range(2):
            mixed_ref[i, part * beams:(part + 1) * beams, :] = lax.dot_general(
                at, x_ref[part], (((0,), (0,)), ((), ())), preferred_element_type=F32
            ).astype(BF16)


def rotate_sum(sp_ref, m_ref, rot_ref, rc_ref, mixed_ref):
    beams = rot_ref.shape[2]
    real = imag = None
    for i in range(2):
        side = i ^ sp_ref[0]
        filtered = jnp.dot(mixed_ref[i], m_ref[side], preferred_element_type=F32)
        fr, fi = filtered[:beams], filtered[beams:]
        cb = jnp.concatenate([rot_ref[side, 0]] * (TILE // 128), axis=1)
        sb = jnp.concatenate([rot_ref[side, 1]] * (TILE // 128), axis=1)
        rc = rc_ref[0, side]
        cr, sr = rc[0:1], rc[1:2]
        cosine = cb * cr - sb * sr
        sine = sb * cr + cb * sr
        re = fr * cosine - fi * sine
        im = fr * sine + fi * cosine
        real = re if real is None else real + re
        imag = im if imag is None else imag + im
    return real, imag


def merge_kernel(sp_ref, xa_ref, xb_ref, m_ref, at_ref, rot_ref, rc_ref, y_ref, mixed_ref):
    @pl.when(pl.program_id(0) == 0)
    def _():
        mix(sp_ref, (xa_ref, xb_ref), at_ref, mixed_ref)

    real, imag = rotate_sum(sp_ref, m_ref, rot_ref, rc_ref, mixed_ref)
    y_ref[0] = real.astype(y_ref.dtype)
    y_ref[1] = imag.astype(y_ref.dtype)


def final_kernel(
    sp_ref, xa_ref, xb_ref, m_ref, at_ref, rot_ref, rc_ref, acc_ref, *rest
):
    y_refs, mixed_ref = rest[:-1], rest[-1]
    step = pl.program_id(0)

    @pl.when(step == 0)
    def _():
        mix(sp_ref, (xa_ref, xb_ref), at_ref, mixed_ref)

    real, imag = rotate_sum(sp_ref, m_ref, rot_ref, rc_ref, mixed_ref)
    real = real + acc_ref[0]
    imag = imag + acc_ref[1]
    for k, y_ref in enumerate(y_refs):

        @pl.when(step == k)
        def _():
            y_ref[0] = real.astype(y_ref.dtype)
            y_ref[1] = imag.astype(y_ref.dtype)


def merge(sp, xa, xb, built, rc, out_dtype=BF16, acc=None):
    m, at, rot = built
    bins = m.shape[1]
    beams = at.shape[1]
    tiles = bins // TILE
    whole = pl.BlockSpec((2, beams, bins), lambda j, sp: (0, 0, 0))

    def col(j, sp):
        return (j + sp[2]) % tiles

    in_specs = [
        whole,
        whole,
        pl.BlockSpec((2, bins, TILE), lambda j, sp: (0, 0, col(j, sp))),
        pl.BlockSpec((2, beams, beams), lambda j, sp: (0, 0, 0)),
        pl.BlockSpec((2, 2, beams, 128), lambda j, sp: (0, 0, 0, 0)),
        pl.BlockSpec((1, 2, 2, TILE), lambda j, sp: (sp[1], 0, 0, col(j, sp))),
    ]
    args = [xa, xb, m, at, rot, rc]
    if acc is None:
        kernel = merge_kernel
        out_specs = pl.BlockSpec((2, beams, TILE), lambda j, sp: (0, 0, col(j, sp)))
        out_shape = jax.ShapeDtypeStruct((2, beams, bins), out_dtype)
    else:
        kernel = final_kernel
        in_specs.append(pl.BlockSpec((2, beams, TILE), lambda j, sp: (0, 0, col(j, sp))))
        args.append(acc)
        out_specs = [pl.BlockSpec((2, beams, TILE), lambda j, sp: (0, 0, 0))] * tiles
        out_shape = [jax.ShapeDtypeStruct((2, beams, TILE), out_dtype)] * tiles
    return pl.pallas_call(
        kernel,
        grid_spec=pltpu.PrefetchScalarGridSpec(
            num_scalar_prefetch=1,
            grid=(tiles,),
            in_specs=in_specs,
            out_specs=out_specs,
            scratch_shapes=[pltpu.VMEM((2, 2 * beams, bins), BF16)],
        ),
        out_shape=out_shape,
        cost_estimate=pl.CostEstimate(
            flops=4 * 2 * beams * bins * (beams + bins), transcendentals=0, bytes_accessed=9 << 20
        ),
        name="merge",
    )(sp, *args)


def local(echoes, angle_offsets, angle_coefs, range_offsets, range_coefs, beam_phase, range_phase):
    levels = lax.axis_size("sub").bit_length() - 1
    n_chan = lax.axis_size("chan")
    device = lax.axis_index("sub")
    share = lax.axis_index("chan")
    sections = angle_offsets.shape[1]
    channels = echoes.shape[1]
    bins = echoes.shape[3]
    units = [echoes[:, c] for c in range(channels)]
    packs = pack_tables(range_coefs, range_offsets, angle_coefs, angle_offsets, beam_phase)
    rc = jnp.stack([jnp.cos(range_phase), jnp.sin(range_phase)], axis=3)
    rc = rc.reshape(channels * sections, 2, 2, bins)
    for section in range(sections):
        bit_pos = levels - 1 - section
        own_bit = device >> bit_pos & 1
        built = build(packs[section])
        partners = [partner_2(u, "sub", bit_pos) for u in units]
        final = section == sections - 1
        acc = None
        new = []
        for c in range(channels):
            sp = jnp.stack([own_bit, c * sections + section, share if final and c else 0]).astype(
                jnp.int32
            )
            if final and c:
                acc = merge(sp, units[c], partners[c], built, rc, BF16, acc)
            elif final:
                acc = merge(sp, units[c], partners[c], built, rc, F32)
            else:
                new.append(merge(sp, units[c], partners[c], built, rc))
        units = new
    image = acc[0].astype(F32)
    for step in range(1, n_chan):
        got = lax.ppermute(acc[step], "chan", [(i, (i + step) % n_chan) for i in range(n_chan)])
        image = image + got.astype(F32)
    return image


def solution(mesh):
    return jax.shard_map(
        local,
        mesh=mesh,
        in_specs=(
            P(None, "chan", "sub", None),
            P("sub", None, None, None),
            P("sub", None, None, None, None),
            P("sub", None, None, None),
            P("sub", None, None, None, None),
            P("sub", None, None, None),
            P("chan", None, None, None),
        ),
        out_specs=P(None, "sub", "chan"),
        check_vma=False,
    )
```

```python
import functools

import jax
import jax.numpy as jnp
from jax import lax
from jax.experimental import pallas as pl
from jax.experimental.pallas import tpu as pltpu
from jax.sharding import PartitionSpec as P


F32 = jnp.float32
BF16 = jnp.bfloat16
TILE = 256
PACK_ROWS = 48


def partner_2(shard, axis, distance):
    return lax.ppermute(shard, axis, [(i, i ^ 1 << distance) for i in range(lax.axis_size(axis))])


def pack_kernel(rc_ref, ro_ref, ac_ref, ao_ref, bp_ref, out_ref):
    sides, taps, bins = rc_ref.shape[2:]
    beams = ac_ref.shape[4]
    spot = lax.broadcasted_iota(jnp.int32, (8, bins), 0)
    for side in range(sides):
        out_ref[side, :taps, :] = rc_ref[0, 0, side].astype(BF16)
        ro = ro_ref[0, 0, side:side + 1, :]
        ao = ao_ref[0, 0, side:side + 1, :]
        beta = bp_ref[0, 0, side:side + 1, :]
        b1 = beta.astype(BF16).astype(F32)
        b2 = (beta - b1).astype(BF16).astype(F32)
        b3 = beta - b1 - b2
        r_hi, r_lo = (ro >> 5).astype(F32), (ro & 31).astype(F32)
        a_hi, a_lo = (ao >> 5).astype(F32), (ao & 31).astype(F32)
        row2 = jnp.concatenate([a_hi, a_lo, b1, b2], axis=1)
        row3 = jnp.concatenate([b3, jnp.zeros((1, bins - beams), F32)], axis=1)
        head = jnp.where(
            spot == 0, r_hi, jnp.where(spot == 1, r_lo, jnp.where(spot == 2, row2, row3))
        )
        angle = jnp.concatenate(
            [ac_ref[0, 0, side, 8 * g:8 * g + 8, :] for g in range(4)], axis=1
        )
        out_ref[side, taps:, :] = jnp.concatenate([head, angle], axis=0).astype(BF16)


def pack_tables(range_coefs, range_offsets, angle_coefs, angle_offsets, beam_phase):
    sections, sides, taps, bins = range_coefs.shape[1:]
    args = (range_coefs, range_offsets, angle_coefs, angle_offsets, beam_phase)

    def spec(a, section):
        index = (0, section) + (0,) * (a.ndim - 2)
        return pl.BlockSpec((1, 1) + a.shape[2:], lambda i: index)

    return [
        pl.pallas_call(
            pack_kernel,
            grid=(1,),
            in_specs=[spec(a, section) for a in args],
            out_specs=pl.BlockSpec((sides, PACK_ROWS, bins), lambda i: (0, 0, 0)),
            out_shape=jax.ShapeDtypeStruct((sides, PACK_ROWS, bins), BF16),
            compiler_params=pltpu.CompilerParams(vmem_limit_bytes=8 << 20),
            name="pack",
        )(*args)
        for section in range(sections)
    ]


def place(taps, hi, lo, blocks, store):
    window = jnp.concatenate([taps, jnp.zeros_like(taps)], axis=0)
    for bit in range(5):
        moved = pltpu.roll(window, 1 << bit, axis=0)
        window = jnp.where((lo >> bit) & 1 == 1, moved, window)
    first, second = window[:32], window[32:]
    hi = jnp.broadcast_to(hi, first.shape)
    zero = jnp.zeros_like(first)
    for k in range(blocks):
        rows = jnp.where(hi == k, first, jnp.where(hi == k - 1, second, zero))
        store(k, rows.astype(BF16))


def build_kernel(pack_ref, m_ref, at_ref, rot_ref):
    bins = m_ref.shape[2]
    beams = at_ref.shape[2]

    def columns(j, carry):
        lanes = pl.ds(pl.multiple_of(j * 128, 128), 128)
        taps = pack_ref[0, :32, lanes].astype(F32)
        head = pack_ref[0, 32:48, lanes].astype(F32)
        hi = head[0:1].astype(jnp.int32)
        lo = head[1:2].astype(jnp.int32)

        def store(k, rows):
            m_ref[0, 32 * k:32 * k + 32, lanes] = rows

        place(taps, hi, lo, bins // 32, store)
        return carry

    lax.fori_loop(0, bins // 128, columns, 0)

    tail = pack_ref[0, 32:48, :].astype(F32)
    angle = jnp.concatenate([tail[8:16, 256 * g:256 * g + 256] for g in range(4)], axis=0)
    a_hi = tail[2:3, 0:256].astype(jnp.int32)
    a_lo = tail[2:3, 256:512].astype(jnp.int32)

    def store_angle(k, rows):
        at_ref[0, 32 * k:32 * k + 32, :] = rows

    place(angle, a_hi, a_lo, beams // 32, store_angle)
    beta = tail[2:3, 512:768] + tail[2:3, 768:1024] + tail[3:4, 0:256]
    beta = jnp.broadcast_to(beta, (8, beams))
    for t, fn in enumerate((jnp.cos, jnp.sin)):
        wide = jnp.broadcast_to(fn(beta)[0:1], (128, beams))
        rot_ref[0, t] = wide.T


def build(pack):
    sides, rows, bins = pack.shape
    beams = 256
    return pl.pallas_call(
        build_kernel,
        grid=(sides,),
        in_specs=[pl.BlockSpec((1, rows, bins), lambda i: (i, 0, 0))],
        out_specs=[
            pl.BlockSpec((1, bins, bins), lambda i: (i, 0, 0)),
            pl.BlockSpec((1, beams, beams), lambda i: (i, 0, 0)),
            pl.BlockSpec((1, 2, beams, 128), lambda i: (i, 0, 0, 0)),
        ],
        out_shape=[
            jax.ShapeDtypeStruct((sides, bins, bins), BF16),
            jax.ShapeDtypeStruct((sides, beams, beams), BF16),
            jax.ShapeDtypeStruct((sides, 2, beams, 128), F32),
        ],
        compiler_params=pltpu.CompilerParams(vmem_limit_bytes=12 << 20),
        name="build",
    )(pack)


def merge_kernel(at_row, with_acc, sp_ref, xa_ref, xb_ref, m_ref, at_ref, rot_ref, rc_ref, *rest):
    mixed_ref = rest[-1]
    acc_ref = rest[0] if with_acc else None
    y_refs = rest[1:-1] if with_acc else rest[:-1]
    beams = rot_ref.shape[2]
    flip, rc_row, turn = sp_ref[at_row], sp_ref[at_row + 1], sp_ref[at_row + 2]
    for i, x_ref in enumerate((xa_ref, xb_ref)):
        at = at_ref[i ^ flip]
        for part in range(2):
            mixed_ref[i, part * beams:(part + 1) * beams, :] = lax.dot_general(
                at, x_ref[part], (((0,), (0,)), ((), ())), preferred_element_type=F32
            ).astype(BF16)
    tiles = m_ref.shape[2] // TILE
    for j in range(tiles):
        if len(y_refs) > 1:
            lanes = pl.ds(pl.multiple_of((j + turn) % tiles * TILE, TILE), TILE)
        else:
            lanes = slice(TILE * j, TILE * (j + 1))
        real = imag = None
        for i in range(2):
            side = i ^ flip
            filtered = jnp.dot(mixed_ref[i], m_ref[side, :, lanes], preferred_element_type=F32)
            fr, fi = filtered[:beams], filtered[beams:]
            cb = jnp.concatenate([rot_ref[side, 0]] * (TILE // 128), axis=1)
            sb = jnp.concatenate([rot_ref[side, 1]] * (TILE // 128), axis=1)
            rc = rc_ref[rc_row, side, :, lanes]
            cr, sr = rc[0:1], rc[1:2]
            cosine = cb * cr - sb * sr
            sine = sb * cr + cb * sr
            re = fr * cosine - fi * sine
            im = fr * sine + fi * cosine
            real = re if real is None else real + re
            imag = im if imag is None else imag + im
        if with_acc:
            real = real + acc_ref[0, :, lanes].astype(F32)
            imag = imag + acc_ref[1, :, lanes].astype(F32)
        if len(y_refs) > 1:
            y_refs[j][0] = real.astype(y_refs[j].dtype)
            y_refs[j][1] = imag.astype(y_refs[j].dtype)
        else:
            y_refs[0][0, :, lanes] = real.astype(y_refs[0].dtype)
            y_refs[0][1, :, lanes] = imag.astype(y_refs[0].dtype)


def merge(sp, at_row, xa, xb, built, rc, out_dtype=BF16, acc=None, split=False):
    m, at, rot = built
    bins = m.shape[1]
    beams = at.shape[1]
    args = [xa, xb, m, at, rot, rc] + ([] if acc is None else [acc])
    vmem = pl.BlockSpec(memory_space=pltpu.VMEM)
    if split:
        out = [jax.ShapeDtypeStruct((2, beams, TILE), out_dtype)] * (bins // TILE)
    else:
        out = [jax.ShapeDtypeStruct((2, beams, bins), out_dtype)]
    got = pl.pallas_call(
        functools.partial(merge_kernel, at_row, acc is not None),
        in_specs=[pl.BlockSpec(memory_space=pltpu.SMEM)] + [vmem] * len(args),
        out_specs=[vmem] * len(out),
        out_shape=out,
        scratch_shapes=[pltpu.VMEM((2, 2 * beams, bins), BF16)],
        compiler_params=pltpu.CompilerParams(vmem_limit_bytes=24 << 20),
        cost_estimate=pl.CostEstimate(
            flops=4 * 2 * beams * bins * (beams + bins), transcendentals=0, bytes_accessed=9 << 20
        ),
        name="merge",
    )(sp, *args)
    return got if split else got[0]


def local(echoes, angle_offsets, angle_coefs, range_offsets, range_coefs, beam_phase, range_phase):
    levels = lax.axis_size("sub").bit_length() - 1
    n_chan = lax.axis_size("chan")
    device = lax.axis_index("sub")
    share = lax.axis_index("chan")
    sections = angle_offsets.shape[1]
    channels = echoes.shape[1]
    bins = echoes.shape[3]
    units = [echoes[:, c] for c in range(channels)]
    packs = pack_tables(range_coefs, range_offsets, angle_coefs, angle_offsets, beam_phase)
    rc = jnp.stack([jnp.cos(range_phase), jnp.sin(range_phase)], axis=3)
    rc = rc.reshape(channels * sections, 2, 2, bins)
    rows = []
    for section in range(sections):
        own_bit = device >> levels - 1 - section & 1
        for c in range(channels):
            rows += [own_bit, jnp.int32(c * sections + section), share]
    sp = jnp.stack(rows).astype(jnp.int32)
    for section in range(sections):
        bit_pos = levels - 1 - section
        built = build(packs[section])
        partners = [partner_2(u, "sub", bit_pos) for u in units]
        final = section == sections - 1
        acc = None
        new = []
        for c in range(channels):
            at_row = 3 * (section * channels + c)
            args = (sp, at_row, units[c], partners[c], built, rc)
            if final and c:
                acc = merge(*args, BF16, acc, True)
            elif final:
                acc = merge(*args, F32)
            else:
                new.append(merge(*args))
        units = new
    image = acc[0].astype(F32)
    for step in range(1, n_chan):
        got = lax.ppermute(acc[step], "chan", [(i, (i + step) % n_chan) for i in range(n_chan)])
        image = image + got.astype(F32)
    return image


def solution(mesh):
    return jax.shard_map(
        local,
        mesh=mesh,
        in_specs=(
            P(None, "chan", "sub", None),
            P("sub", None, None, None),
            P("sub", None, None, None, None),
            P("sub", None, None, None),
            P("sub", None, None, None, None),
            P("sub", None, None, None),
            P("chan", None, None, None),
        ),
        out_specs=P(None, "sub", "chan"),
        check_vma=False,
    )
```

```python
import functools

import jax
import jax.numpy as jnp
from jax import lax
from jax.experimental import pallas as pl
from jax.experimental.pallas import tpu as pltpu
from jax.sharding import PartitionSpec as P


F32 = jnp.float32
BF16 = jnp.bfloat16
TILE = 256
PACK_ROWS = 48


def move(array, to):
    n_sub, n_chan = lax.axis_size("sub"), lax.axis_size("chan")
    pairs = []
    for sub in range(n_sub):
        for share in range(n_chan):
            k5, k4, k3, core = sub >> 5 & 1, sub >> 4 & 1, sub >> 3 & 1, sub & 1
            k5, k4, k3, core, shift = to(k5, k4, k3, core)
            dest = k5 << 5 | k4 << 4 | k3 << 3 | (sub & 6) | core
            pairs.append((sub * n_chan + share, dest * n_chan + (share + shift) % n_chan))
    return lax.ppermute(array, ("sub", "chan"), pairs)


def pack_kernel(rc_ref, ro_ref, ac_ref, ao_ref, bp_ref, out_ref):
    sides, taps, bins = rc_ref.shape[2:]
    beams = ac_ref.shape[4]
    spot = lax.broadcasted_iota(jnp.int32, (8, bins), 0)
    for side in range(sides):
        out_ref[side, :taps, :] = rc_ref[0, 0, side].astype(BF16)
        ro = ro_ref[0, 0, side:side + 1, :]
        ao = ao_ref[0, 0, side:side + 1, :]
        beta = bp_ref[0, 0, side:side + 1, :]
        b1 = beta.astype(BF16).astype(F32)
        b2 = (beta - b1).astype(BF16).astype(F32)
        b3 = beta - b1 - b2
        r_hi, r_lo = (ro >> 5).astype(F32), (ro & 31).astype(F32)
        a_hi, a_lo = (ao >> 5).astype(F32), (ao & 31).astype(F32)
        row2 = jnp.concatenate([a_hi, a_lo, b1, b2], axis=1)
        row3 = jnp.concatenate([b3, jnp.zeros((1, bins - beams), F32)], axis=1)
        head = jnp.where(
            spot == 0, r_hi, jnp.where(spot == 1, r_lo, jnp.where(spot == 2, row2, row3))
        )
        angle = jnp.concatenate(
            [ac_ref[0, 0, side, 8 * g:8 * g + 8, :] for g in range(4)], axis=1
        )
        out_ref[side, taps:, :] = jnp.concatenate([head, angle], axis=0).astype(BF16)


def pack_tables(range_coefs, range_offsets, angle_coefs, angle_offsets, beam_phase):
    sections, sides, taps, bins = range_coefs.shape[1:]
    args = (range_coefs, range_offsets, angle_coefs, angle_offsets, beam_phase)

    def spec(a, section):
        index = (0, section) + (0,) * (a.ndim - 2)
        return pl.BlockSpec((1, 1) + a.shape[2:], lambda i: index)

    return [
        pl.pallas_call(
            pack_kernel,
            grid=(1,),
            in_specs=[spec(a, section) for a in args],
            out_specs=pl.BlockSpec((sides, PACK_ROWS, bins), lambda i: (0, 0, 0)),
            out_shape=jax.ShapeDtypeStruct((sides, PACK_ROWS, bins), BF16),
            compiler_params=pltpu.CompilerParams(vmem_limit_bytes=8 << 20),
            name="pack",
        )(*args)
        for section in range(sections)
    ]


def place(taps, hi, lo, blocks, store):
    window = jnp.concatenate([taps, jnp.zeros_like(taps)], axis=0)
    for bit in range(5):
        moved = pltpu.roll(window, 1 << bit, axis=0)
        window = jnp.where((lo >> bit) & 1 == 1, moved, window)
    first, second = window[:32], window[32:]
    hi = jnp.broadcast_to(hi, first.shape)
    zero = jnp.zeros_like(first)
    for k in range(blocks):
        rows = jnp.where(hi == k, first, jnp.where(hi == k - 1, second, zero))
        store(k, rows.astype(BF16))


def build_kernel(at_row, sp_ref, pa_ref, pb_ref, m_ref, at_ref, rot_ref):
    side = pl.program_id(0)
    bins = m_ref.shape[2]
    beams = at_ref.shape[2]
    first = sp_ref[at_row] == 0

    def columns(j, carry):
        lanes = pl.ds(pl.multiple_of(j * 128, 128), 128)
        both = jnp.where(
            first, pa_ref[side, :, lanes].astype(F32), pb_ref[side, :, lanes].astype(F32)
        )
        hi = both[32:33].astype(jnp.int32)
        lo = both[33:34].astype(jnp.int32)

        def store(k, rows):
            m_ref[0, 32 * k:32 * k + 32, lanes] = rows

        place(both[:32], hi, lo, bins // 32, store)
        return carry

    lax.fori_loop(0, bins // 128, columns, 0)

    tail = jnp.where(
        first, pa_ref[side, 32:48, :].astype(F32), pb_ref[side, 32:48, :].astype(F32)
    )
    angle = jnp.concatenate([tail[8:16, 256 * g:256 * g + 256] for g in range(4)], axis=0)
    a_hi = tail[2:3, 0:256].astype(jnp.int32)
    a_lo = tail[2:3, 256:512].astype(jnp.int32)

    def store_angle(k, rows):
        at_ref[0, 32 * k:32 * k + 32, :] = rows

    place(angle, a_hi, a_lo, beams // 32, store_angle)
    beta = tail[2:3, 512:768] + tail[2:3, 768:1024] + tail[3:4, 0:256]
    beta = jnp.broadcast_to(beta, (8, beams))
    for t, fn in enumerate((jnp.cos, jnp.sin)):
        wide = jnp.broadcast_to(fn(beta)[0:1], (128, beams))
        rot_ref[0, t] = wide.T


def build(sp, at_row, pack_a, pack_b):
    sides, rows, bins = pack_a.shape
    beams = bins // 4
    whole = pl.BlockSpec((sides, rows, bins), lambda i: (0, 0, 0))
    return pl.pallas_call(
        functools.partial(build_kernel, at_row),
        grid=(sides,),
        in_specs=[pl.BlockSpec(memory_space=pltpu.SMEM), whole, whole],
        out_specs=[
            pl.BlockSpec((1, bins, bins), lambda i: (i, 0, 0)),
            pl.BlockSpec((1, beams, beams), lambda i: (i, 0, 0)),
            pl.BlockSpec((1, 2, beams, 128), lambda i: (i, 0, 0, 0)),
        ],
        out_shape=[
            jax.ShapeDtypeStruct((sides, bins, bins), BF16),
            jax.ShapeDtypeStruct((sides, beams, beams), BF16),
            jax.ShapeDtypeStruct((sides, 2, beams, 128), F32),
        ],
        compiler_params=pltpu.CompilerParams(vmem_limit_bytes=12 << 20),
        name="build",
    )(sp, pack_a, pack_b)


def merge_kernel(at_row, with_acc, sp_ref, xa_ref, xb_ref, m_ref, at_ref, rot_ref, rc_ref, *rest):
    mixed_ref = rest[-1]
    acc_ref = rest[0] if with_acc else None
    y_refs = rest[1:-1] if with_acc else rest[:-1]
    beams = rot_ref.shape[2]
    flip, rc_row, turn = sp_ref[at_row], sp_ref[at_row + 1], sp_ref[at_row + 2]
    for i, x_ref in enumerate((xa_ref, xb_ref)):
        at = at_ref[i ^ flip]
        for part in range(2):
            mixed_ref[i, part * beams:(part + 1) * beams, :] = lax.dot_general(
                at, x_ref[part], (((0,), (0,)), ((), ())), preferred_element_type=F32
            ).astype(BF16)
    tiles = m_ref.shape[2] // TILE
    for j in range(tiles):
        if len(y_refs) > 1:
            lanes = pl.ds(pl.multiple_of((j + turn) % tiles * TILE, TILE), TILE)
        else:
            lanes = slice(TILE * j, TILE * (j + 1))
        real = imag = None
        for i in range(2):
            side = i ^ flip
            filtered = jnp.dot(mixed_ref[i], m_ref[side, :, lanes], preferred_element_type=F32)
            fr, fi = filtered[:beams], filtered[beams:]
            cb = jnp.concatenate([rot_ref[side, 0]] * (TILE // 128), axis=1)
            sb = jnp.concatenate([rot_ref[side, 1]] * (TILE // 128), axis=1)
            rc = rc_ref[rc_row, side, :, lanes]
            cr, sr = rc[0:1], rc[1:2]
            cosine = cb * cr - sb * sr
            sine = sb * cr + cb * sr
            re = fr * cosine - fi * sine
            im = fr * sine + fi * cosine
            real = re if real is None else real + re
            imag = im if imag is None else imag + im
        if with_acc:
            real = real + acc_ref[0, :, lanes].astype(F32)
            imag = imag + acc_ref[1, :, lanes].astype(F32)
        if len(y_refs) > 1:
            y_refs[j][0] = real.astype(y_refs[j].dtype)
            y_refs[j][1] = imag.astype(y_refs[j].dtype)
        else:
            y_refs[0][0, :, lanes] = real.astype(y_refs[0].dtype)
            y_refs[0][1, :, lanes] = imag.astype(y_refs[0].dtype)


def merge(sp, at_row, xa, xb, built, rc, out_dtype=BF16, acc=None, split=False):
    m, at, rot = built
    bins = m.shape[1]
    beams = at.shape[1]
    args = [xa, xb, m, at, rot, rc] + ([] if acc is None else [acc])
    vmem = pl.BlockSpec(memory_space=pltpu.VMEM)
    if split:
        out = [jax.ShapeDtypeStruct((2, beams, TILE), out_dtype)] * (bins // TILE)
    else:
        out = [jax.ShapeDtypeStruct((2, beams, bins), out_dtype)]
    got = pl.pallas_call(
        functools.partial(merge_kernel, at_row, acc is not None),
        in_specs=[pl.BlockSpec(memory_space=pltpu.SMEM)] + [vmem] * len(args),
        out_specs=[vmem] * len(out),
        out_shape=out,
        scratch_shapes=[pltpu.VMEM((2, 2 * beams, bins), BF16)],
        compiler_params=pltpu.CompilerParams(vmem_limit_bytes=24 << 20),
        cost_estimate=pl.CostEstimate(
            flops=4 * 2 * beams * bins * (beams + bins), transcendentals=0, bytes_accessed=9 << 20
        ),
        name="merge",
    )(sp, *args)
    return got if split else got[0]


def local(echoes, angle_offsets, angle_coefs, range_offsets, range_coefs, beam_phase, range_phase):
    device = lax.axis_index("sub")
    share = lax.axis_index("chan")
    n_chan = lax.axis_size("chan")
    sections = angle_offsets.shape[1]
    channels = echoes.shape[1]
    bins = echoes.shape[3]
    k5, k4, k3, core = (device >> bit & 1 for bit in (5, 4, 3, 0))
    sp = jnp.stack([
        1 ^ core ^ k4, core ^ k4, k3 ^ k4, 1 ^ k3 ^ k4, 1 + 0 * core, 0 * core,
        k4, k4 * sections, 0 * core,
        core, k4 * sections + 1, 0 * core,
        k4, core * sections + 2, share,
    ]).astype(jnp.int32)
    packs = pack_tables(range_coefs, range_offsets, angle_coefs, angle_offsets, beam_phase)
    rc = jnp.stack([jnp.cos(range_phase), jnp.sin(range_phase)], axis=3)
    rc = rc.reshape(channels * sections, 2, 2, bins)

    def gather(i):
        return lambda k5, k4, k3, core: (core, i ^ k5, k3, k4, 0)

    def gather_next(i):
        return lambda k5, k4, k3, core: (core, i ^ k4, k3, k5, 0)

    def gather_last(i):
        return lambda k5, k4, k3, core: (k5, k4, core ^ k4, k3 ^ i, 0)

    def spread(i):
        return lambda k5, k4, k3, core: (core, i ^ k3, k5 ^ i ^ k3, k4, 0)

    def swap(k5, k4, k3, core):
        return (k5, k4, k3, 1 ^ core, 0)

    def home(shift):
        return lambda k5, k4, k3, core: (k5, k4, core, k3 ^ k4, shift)

    tables = [move(packs[0], gather(i)) for i in range(2)]
    units = [
        move(lax.dynamic_index_in_dim(echoes, i ^ k5, 1, keepdims=False), gather(i))
        for i in range(2)
    ]
    pack1, pack2, units[0], units[1] = lax.optimization_barrier(
        (packs[1], packs[2], units[0], units[1])
    )
    tables1 = [move(pack1, gather_next(i)) for i in range(2)]
    tables2 = [move(pack2, gather_last(i)) for i in range(2)]

    given = merge(sp, 6, *units, build(sp, 0, *tables), rc)
    kept = merge(sp, 6, *units, build(sp, 1, *tables), rc)
    pair = (kept, move(given, swap))
    units = [
        move(merge(sp, 9, *pair, build(sp, 2 + i, *tables1), rc), spread(i)) for i in range(2)
    ]
    given = merge(sp, 12, *units, build(sp, 4, *tables2), rc)
    parts = merge(sp, 12, *units, build(sp, 5, *tables2), rc, BF16, move(given, swap), True)
    image = None
    for step in range(n_chan):
        got = move(parts[step], home(step)).astype(F32)
        image = got if image is None else image + got
    return image


def solution(mesh):
    return jax.shard_map(
        local,
        mesh=mesh,
        in_specs=(
            P(None, "chan", "sub", None),
            P("sub", None, None, None),
            P("sub", None, None, None, None),
            P("sub", None, None, None),
            P("sub", None, None, None, None),
            P("sub", None, None, None),
            P("chan", None, None, None),
        ),
        out_specs=P(None, "sub", "chan"),
        check_vma=False,
    )
```
